32 devices in a mesh: row: 4 (over y, core), col: 8 (over z, x).
Axes of the slice: x: 2, y: 2, z: 4, core: 2. Of those that a mesh axis runs over, the one named last changes fastest.
Arguments:
- objects: float32 [2, 2, 1024, 2048], P(None, None, 'row', 'col'), may hold values from -5 to 5
- probe: float32 [2, 256, 256], replicated, may hold values from -6 to 6
- prev_partial: float32 [4, 8, 2, 256, 256], P('row', 'col'), may hold values from -6 to 6
- offsets: int32 [4, 8, 1, 2], P('row', 'col'), may hold values from 0 to 128
- counts: int32 [4, 8], P('row', 'col'), may hold values from 0 to 1
- amplitudes: float32 [4, 8, 1, 256, 256], P('row', 'col'), may hold values from 1 to 2.5
Outputs:
- new_objects: float32 [2, 2, 1024, 2048], P(None, None, 'row', 'col')
- new_probe: float32 [2, 256, 256], replicated
- new_partial: float32 [4, 8, 2, 256, 256], P('row', 'col')
The draws below stay inside these ranges and needn't reach their ends.
All inputs are finite; a program needn't handle non-finite values.
Results may differ from the reference program's by a relative error of at most 0.0003.
Values sent between devices are 32-bit elements; how exact they have to be, the bound alone decides.
A program may use at most 64 MiB of HBM per device.

```python
import math
import jax
import jax.numpy as jnp
from jax import lax

WIN = 256
HALO = 64
TILE = 256
PAT = 1
NY = 1024
NX = 2048
N_ROW = 4
N_COL = 8


def with_ends(drawn, stream_key, low, top_value):
    shape = drawn.shape
    place = [jax.random.randint(jax.random.fold_in(stream_key, axis), (), 0, shape[axis]) for axis in range(len(shape))]
    drawn = drawn.at[tuple(place)].set(low)
    longest = shape.index(max(shape))
    place[longest] = (place[longest] + 1) % shape[longest]
    return drawn.at[tuple(place)].set(top_value)


def shard_levels(stream_key, shape, shards, least, high):
    def one(dim, parts):
        draws = jax.random.uniform(jax.random.fold_in(jax.random.fold_in(stream_key, 6), dim), (parts,), jnp.float32, least / len(shards), high / len(shards))
        return jnp.repeat(jnp.exp(draws), shape[dim] // parts).reshape((-1,) + (1,) * (len(shape) - dim - 1))

    level = one(*shards[0])
    for cut in shards[1:]:
        level = level * one(*cut)
    return level


def gaussian(own_key, shape, scale, limit, pieces=(), held_as=jnp.bfloat16):
    array = scale * jax.random.normal(own_key, shape, jnp.float32)
    if pieces:
        array = array * shard_levels(own_key, shape, pieces, -0.22, 0.18)
    return jnp.clip(array, -limit, limit).astype(held_as)


def setup_inputs(seed: int = 0) -> dict:
    key_of = jax.random.split(jax.random.key(seed), 7)
    return {
        "objects": gaussian(key_of[0], (2, 2, NY, NX), 0.7, 5.0, ((2, 4), (3, 8)), jnp.float32),
        "probe": gaussian(key_of[1], (2, WIN, WIN), 1.0, 6.0, (), jnp.float32),
        "prev_partial": gaussian(key_of[2], (N_ROW, N_COL, 2, WIN, WIN), 1.0, 6.0, ((0, 4), (1, 8)), jnp.float32),
        "offsets": with_ends(jax.random.randint(key_of[3], (N_ROW, N_COL, PAT, 2), 0, TILE + 2 * HALO - WIN + 1), jax.random.fold_in(key_of[3], 1), 0, TILE + 2 * HALO - WIN).astype(jnp.int32),
        "counts": with_ends(jax.random.randint(key_of[4], (N_ROW, N_COL), 0, PAT + 1), jax.random.fold_in(key_of[4], 1), 0, PAT).astype(jnp.int32),
        "amplitudes": jnp.clip(1.0 + 1.5 * jax.random.uniform(key_of[5], (N_ROW, N_COL, PAT, WIN, WIN), jnp.float32) ** shard_levels(key_of[5], (N_ROW, N_COL, PAT, WIN, WIN), ((0, 4), (1, 8)), -0.2, 0.2), 1.0, 2.5),
    }


OBJ_RATE = 0.1
PROBE_RATE = 0.3

def fresnel(n):
    index = jnp.arange(n, dtype=jnp.int32)
    freq = jnp.where(index < n // 2, index, index - n)
    square = (freq * freq).astype(jnp.float32)
    phase = jnp.pi * (square[:, None] + square[None, :]) / (4.0 * n)
    return (jnp.cos(phase), jnp.sin(phase))

def pattern_loss(ext, probe, offset, live, amp):
    zero = jnp.zeros((), jnp.int32)
    window = lax.dynamic_slice(ext, (zero, zero, offset[0].astype(jnp.int32), offset[1].astype(jnp.int32)), (2, 2, WIN, WIN))
    first = lax.complex(window[0, 0], window[0, 1])
    second = lax.complex(window[1, 0], window[1, 1])
    wave = lax.complex(probe[0], probe[1]) * first
    hre, him = fresnel(WIN)
    spectrum = jnp.fft.fft2(wave, norm='ortho') * lax.complex(hre, him)
    wave = jnp.fft.ifft2(spectrum, norm='ortho') * second
    far = jnp.fft.fft2(wave, norm='ortho')
    power = jnp.real(far) ** 2 + jnp.imag(far) ** 2
    return live * jnp.sum((jnp.sqrt(power + 1.0) - amp) ** 2)

def local_grads(ext, probe, offsets, count, amps):
    live = (jnp.arange(PAT, dtype=jnp.int32) < count).astype(jnp.float32)

    def total(ext_in, probe_in):
        losses = jax.vmap(pattern_loss, in_axes=(None, None, 0, 0, 0))(ext_in, probe_in, offsets, live, amps)
        return jnp.sum(losses)
    return jax.grad(total, argnums=(0, 1))(ext, probe)

def reference(objects, probe, prev_partial, offsets, counts, amplitudes):
    padded = jnp.pad(objects, ((0, 0), (0, 0), (HALO, HALO), (HALO, HALO)))
    side = TILE + 2 * HALO
    zero = jnp.zeros((), jnp.int32)

    def visit(grad_pad, index):
        tile_row = index // N_COL
        tile_col = index % N_COL
        top = (tile_row * TILE).astype(jnp.int32)
        left = (tile_col * TILE).astype(jnp.int32)
        ext = lax.dynamic_slice(padded, (zero, zero, top, left), (2, 2, side, side))
        grad_ext, grad_probe = local_grads(ext, probe, offsets[tile_row, tile_col], counts[tile_row, tile_col], amplitudes[tile_row, tile_col])
        old = lax.dynamic_slice(grad_pad, (zero, zero, top, left), (2, 2, side, side))
        grad_pad = lax.dynamic_update_slice(grad_pad, old + grad_ext, (zero, zero, top, left))
        return (grad_pad, grad_probe)
    start = jnp.zeros(padded.shape, jnp.float32)
    grad_pad, partials = lax.scan(visit, start, jnp.arange(N_ROW * N_COL, dtype=jnp.int32))
    grad = grad_pad[:, :, HALO:HALO + NY, HALO:HALO + NX]
    new_partial = partials.reshape(N_ROW, N_COL, 2, WIN, WIN)
    total = lax.optimization_barrier(jnp.sum(prev_partial, axis=(0, 1)))
    rate = PROBE_RATE / math.sqrt(N_ROW * N_COL)
    return (objects - OBJ_RATE * grad, probe - rate * total, new_partial)
```

```python
import functools
import math

import jax
import jax.numpy as jnp
import numpy as np
from jax import lax
from jax.experimental import pallas as pl
from jax.experimental.pallas import tpu as pltpu
from jax.sharding import PartitionSpec as P

HALO = 64
OBJ_RATE = 0.1
PROBE_RATE = 0.3
MESH = pl.DeviceIdType.MESH

STEPS = ((-1, 0), (1, 0), (0, -1), (0, 1), (-1, -1), (-1, 1), (1, -1), (1, 1))


def split(value):
    high = value.astype(jnp.bfloat16)
    low = (value - high.astype(jnp.float32)).astype(jnp.bfloat16)
    return high, low


def operator_table(n):
    index = np.arange(n)
    angle = 2.0 * np.pi * (np.outer(index, index) % n) / n
    dft = np.exp(-1j * angle) / np.sqrt(n)
    freq = np.where(index < n // 2, index, index - n).astype(np.float64)
    phase = np.exp(1j * np.pi * freq * freq / (4.0 * n))
    prop = np.conj(dft) @ (phase[:, None] * dft)
    tables = []
    for mat in (dft, prop):
        for part in (mat.real, mat.imag, -mat.imag):
            part = part.astype(np.float32)
            high = part.astype(jnp.bfloat16)
            low = (part - high.astype(np.float32)).astype(jnp.bfloat16)
            tables += [high, low]
    return np.stack(tables).reshape(2, 3, 2, n, n)


def dot(left, right):
    return jnp.dot(left, right, preferred_element_type=jnp.float32)


def cat(parts, axis):
    return jnp.concatenate(parts, axis=axis)


def sandwich(xr, xi, table, which, conj):
    re, im, neg = table.at[which, 0], table.at[which, 1], table.at[which, 2]
    if conj:
        im, neg = neg, im
    rh, rl, ih, il, nh, nl = (p[k] for p in (re, im, neg) for k in (0, 1))
    xrh, xrl = split(xr)
    xih, xil = split(xi)
    left = cat([xrh, xih, xrl, xil, xrh, xih], 1)
    tr = dot(left, cat([rh, nh, rh, nh, rl, nl], 0))
    ti = dot(left, cat([ih, rh, ih, rh, il, rl], 0))
    trh, trl = split(tr)
    tih, til = split(ti)
    right = cat([trh, tih, trl, til, trh, tih], 0)
    yr = dot(cat([rh, nh, rh, nh, rl, nl], 1), right)
    yi = dot(cat([ih, rh, ih, rh, il, rl], 1), right)
    return yr, yi


def kernel(
    rows, cols, offs, count, obj_hbm, prev_hbm, probe_hbm, probe_k_hbm, amp_hbm, table_hbm,
    out_obj, out_probe, out_part,
    obj, prev, probe, probe_piece, amp, table,
    pw, pe, ext, rw, re_,
    acc, gn, gs, gw_, ge, qn, qs, qw, qe,
    buf1, sum1, buf2, newp,
    local_sem, halo_send, halo_recv, row_send, row_recv, col_send, col_recv,
):
    tile = obj.shape[2]
    win = probe.shape[1]
    side = tile + 2 * HALO
    row, col = lax.axis_index("row"), lax.axis_index("col")

    def exists(dr, dc):
        r, c = row + dr, col + dc
        return (r >= 0) & (r < rows) & (c >= 0) & (c < cols)

    fetches = [
        pltpu.make_async_copy(src, dst, local_sem.at[k])
        for k, (src, dst) in enumerate(
            ((obj_hbm, obj), (prev_hbm, prev), (probe_k_hbm.at[row, col], probe_piece),
             (probe_hbm, probe), (table_hbm, table), (amp_hbm, amp))
        )
    ]
    for fetch in fetches:
        fetch.start()

    barrier = pltpu.get_barrier_semaphore()

    def greet(r, c):
        pl.semaphore_signal(barrier, inc=1, device_id=(r, c), device_id_type=MESH)

    for t in range(1, rows):
        greet(lax.rem(row + t, rows), col)
    for t in range(1, cols):
        greet(row, lax.rem(col + t, cols))
    for dr, dc in STEPS[4:]:
        @pl.when(exists(dr, dc))
        def _():
            greet(row + dr, col + dc)

    lane = lax.broadcasted_iota(jnp.int32, (1, 2 * HALO), 1)
    first = lane < HALO

    def swap(value):
        return pltpu.roll(value, HALO, 1)

    fetches[0].wait()
    for s in range(2):
        head_re, head_im = obj[s, 0, :, : 2 * HALO], obj[s, 1, :, : 2 * HALO]
        tail_re, tail_im = obj[s, 0, :, tile - 2 * HALO :], obj[s, 1, :, tile - 2 * HALO :]
        pw[s] = jnp.where(first, head_re, swap(head_im))
        pe[s] = jnp.where(first, swap(tail_re), tail_im)

    north, south = pl.ds(0, HALO), pl.ds(tile + HALO, HALO)
    middle = pl.ds(HALO, tile)
    low, high = pl.ds(0, HALO), pl.ds(tile - HALO, HALO)
    wide = pl.ds(0, tile)

    def halo_plan(s):
        return (
            (obj.at[s, :, low, :], ext.at[s, :, south, wide]),
            (obj.at[s, :, high, :], ext.at[s, :, north, wide]),
            (pw.at[s], re_.at[s, middle]),
            (pe.at[s], rw.at[s, middle]),
            (pw.at[s, low], re_.at[s, south]),
            (pe.at[s, low], rw.at[s, south]),
            (pw.at[s, high], re_.at[s, north]),
            (pe.at[s, high], rw.at[s, north]),
        )

    def grad_plan(s):
        return (
            (gn.at[s], qs.at[s]),
            (gs.at[s], qn.at[s]),
            (gw_.at[s, middle], qe.at[s, middle]),
            (ge.at[s, middle], qw.at[s, middle]),
            (gw_.at[s, north], qe.at[s, south]),
            (ge.at[s, north], qw.at[s, south]),
            (gw_.at[s, south], qe.at[s, north]),
            (ge.at[s, south], qw.at[s, north]),
        )

    def plan_of(phase, s):
        return halo_plan(s) if phase == 0 else grad_plan(s)

    def copies(phase, s):
        plan = plan_of(phase, s)
        return [
            (dr, dc, dst, pltpu.make_async_remote_copy(
                src_ref=src, dst_ref=dst,
                send_sem=halo_send.at[phase, s, d], recv_sem=halo_recv.at[phase, s, d],
                device_id=(row + dr, col + dc), device_id_type=MESH))
            for d, ((dr, dc), (src, dst)) in enumerate(zip(STEPS, plan))
        ]

    order = (2, 3, 4, 5, 6, 7, 0, 1)

    def send(phase, s):
        todo = copies(phase, s)
        for d in order:
            dr, dc, dst, copy = todo[d]

            @pl.when(exists(dr, dc))
            def _():
                copy.start()

    def blank(phase, s):
        for (dr, dc), (_, dst) in zip(STEPS, plan_of(phase, s)):
            @pl.when(jnp.logical_not(exists(-dr, -dc)))
            def _():
                dst[...] = jnp.zeros(dst.shape, jnp.float32)

    def arrive(phase, s):
        for dr, dc, dst, copy in copies(phase, s):
            @pl.when(exists(-dr, -dc))
            def _():
                copy.wait_recv()

    def sent(phase, s):
        for dr, dc, dst, copy in copies(phase, s):
            @pl.when(exists(dr, dc))
            def _():
                copy.wait_send()

    def row_copies(stage):
        made = []
        for t in range(1, rows):
            peer = lax.rem(row + t, rows)
            if stage == 0:
                src, dst = prev.at[peer], buf1.at[t - 1]
            else:
                src, dst = newp.at[row], newp.at[row]
            made.append(pltpu.make_async_remote_copy(
                src_ref=src, dst_ref=dst, send_sem=row_send.at[stage, t - 1],
                recv_sem=row_recv.at[stage, t - 1], device_id=(peer, col), device_id_type=MESH))
        return made

    def col_copies(stage):
        made = []
        for t in range(1, cols):
            peer = lax.rem(col + t, cols)
            if stage == 0:
                src, dst = sum1.at[peer], buf2.at[t - 1]
            else:
                src, dst = newp.at[row, col], newp.at[row, col]
            made.append(pltpu.make_async_remote_copy(
                src_ref=src, dst_ref=dst, send_sem=col_send.at[stage, t - 1],
                recv_sem=col_recv.at[stage, t - 1], device_id=(row, peer), device_id_type=MESH))
        return made

    diagonals = sum(exists(dr, dc).astype(jnp.int32) for dr, dc in STEPS[4:])
    pl.semaphore_wait(barrier, rows - 1 + cols - 1 + diagonals)

    send(0, 0)
    fetches[1].wait()
    rs_rows = row_copies(0)
    for copy in rs_rows:
        copy.start()
    send(0, 1)

    for s in range(2):
        for part in range(2):
            ext[s, part, HALO : HALO + tile, :] = obj[s, part]
        blank(0, s)
        blank(1, s)

    for copy in rs_rows:
        copy.wait_recv()
    total = prev[row]
    for t in range(1, rows):
        total = total + buf1[t - 1]
    sum1[...] = total
    rs_cols = col_copies(0)
    for copy in rs_cols:
        copy.start()

    top, left = offs[0], offs[1]

    def one_hot(shape, axis, shift):
        longer = lax.broadcasted_iota(jnp.int32, shape, axis)
        shorter = lax.broadcasted_iota(jnp.int32, shape, 1 - axis) + shift
        shorter = jnp.where(shorter < 0, shorter + side, shorter)
        return (longer == shorter).astype(jnp.float32).astype(jnp.bfloat16)

    def twice(value, axis):
        return cat([value, value], axis)

    def window(s):
        east, west = re_[s], rw[s]
        full = cat([
            ext[s, 0, :, :tile], jnp.where(first, east, swap(west)),
            ext[s, 1, :, :tile], jnp.where(first, swap(east), west),
        ], 1)
        pick_rows = one_hot((win, side), 1, top)
        pick_cols = one_hot((side, win), 0, left - HALO)
        some = dot(twice(pick_rows, 1), cat(split(full), 0))
        some = cat([some[:, :side], some[:, side:]], 0)
        some = dot(cat(split(some), 1), twice(pick_cols, 0))
        return some[:win], some[win:]

    def place(s, gre, gim):
        put_cols = one_hot((win, side), 1, left - HALO)
        put_rows = one_hot((side, win), 0, top)
        some = dot(cat(split(cat([gre, gim], 0)), 1), twice(put_cols, 0))
        some = cat([some[:win], some[win:]], 1)
        full = dot(twice(put_rows, 1), cat(split(some), 0))
        full_re, full_im = full[:, :side], full[:, side:]
        for part, value in enumerate((full_re, full_im)):
            gn[s, part] = value[:HALO, :tile]
            gs[s, part] = value[HALO + tile :, :tile]
            acc[s, part] = value[HALO : HALO + tile, :tile]
        edge_re, edge_im = full_re[:, tile:], full_im[:, tile:]
        ge[s] = jnp.where(first, edge_re, swap(edge_im))
        gw_[s] = jnp.where(first, swap(edge_re), edge_im)

    arrive(0, 0)
    for k in (3, 4):
        fetches[k].wait()
    ar, ai = window(0)
    pr, pi = probe[0], probe[1]
    vr, vi = sandwich(pr * ar - pi * ai, pr * ai + pi * ar, table, 1, False)

    for copy in rs_cols:
        copy.wait_recv()
    fetches[2].wait()
    total = sum1[col]
    for t in range(1, cols):
        total = total + buf2[t - 1]
    rate = PROBE_RATE / math.sqrt(rows * cols)
    newp[row, col] = probe_piece[...] - rate * total
    ag_cols = col_copies(1)
    for copy in ag_cols:
        copy.start()

    arrive(0, 1)
    br, bi = window(1)
    wr, wi = sandwich(vr * br - vi * bi, vr * bi + vi * br, table, 0, False)
    fetches[5].wait()
    live = jnp.where(count[0] > 0, 2.0, 0.0)
    scale = live * (1.0 - amp[...] / jnp.sqrt(wr * wr + wi * wi + 1.0))
    xr, xi = sandwich(scale * wr, scale * wi, table, 0, True)
    place(1, xr * vr + xi * vi, xi * vr - xr * vi)
    send(1, 1)

    for copy in ag_cols:
        copy.wait_recv()
    ag_rows = row_copies(1)
    for copy in ag_rows:
        copy.start()

    ur, ui = sandwich(xr * br + xi * bi, xi * br - xr * bi, table, 1, True)
    place(0, ur * pr + ui * pi, ui * pr - ur * pi)
    send(1, 0)
    out_part[0] = ur * ar + ui * ai
    out_part[1] = ui * ar - ur * ai

    def finish(s):
        arrive(1, s)
        top_strip, bottom_strip = slice(0, HALO), slice(tile - HALO, tile)
        for part in range(2):
            acc[s, part, top_strip, :] += qn[s, part]
            acc[s, part, bottom_strip, :] += qs[s, part]
        for q, near, lanes in ((qw, True, slice(0, 2 * HALO)), (qe, False, slice(tile - 2 * HALO, tile))):
            for src, dst in (
                (slice(HALO, HALO + tile), slice(0, tile)),
                (slice(0, HALO), top_strip),
                (slice(HALO + tile, side), bottom_strip),
            ):
                value = q[s, src]
                turned = swap(value)
                if near:
                    acc[s, 0, dst, lanes] += jnp.where(first, value, 0.0)
                    acc[s, 1, dst, lanes] += jnp.where(first, turned, 0.0)
                else:
                    acc[s, 0, dst, lanes] += jnp.where(first, 0.0, turned)
                    acc[s, 1, dst, lanes] += jnp.where(first, 0.0, value)
        for part in range(2):
            out_obj[s, part] = obj[s, part] - OBJ_RATE * acc[s, part]

    finish(1)
    for copy in ag_rows:
        copy.wait_recv()
    out_probe[...] = newp[...]
    finish(0)

    for s in range(2):
        sent(0, s)
        sent(1, s)
    for copy in rs_rows + rs_cols + ag_cols + ag_rows:
        copy.wait_send()


def shards(rows, cols, objects, probe, prev_partial, offsets, counts, amplitudes):
    tile = objects.shape[2]
    win = probe.shape[-1]
    side = tile + 2 * HALO
    piece = (2 * win) // (rows * cols)
    split_shape = (rows, cols, piece, win)
    table = jnp.asarray(operator_table(win))
    f32 = jnp.float32
    smem = pl.BlockSpec(memory_space=pltpu.SMEM)
    anyspace = pl.BlockSpec(memory_space=pl.ANY)
    vmem = pl.BlockSpec(memory_space=pltpu.VMEM)
    V = lambda *shape: pltpu.VMEM(shape, f32)
    strip = (2, side, 2 * HALO)
    flat = (2, 2, HALO, tile)
    dma = pltpu.SemaphoreType.DMA
    scratch = [
        V(2, 2, tile, tile), V(*split_shape), V(2, win, win), V(piece, win), V(win, win),
        pltpu.VMEM(table.shape, jnp.bfloat16),
        V(2, tile, 2 * HALO), V(2, tile, 2 * HALO), V(2, 2, side, tile), V(*strip), V(*strip),
        V(2, 2, tile, tile),
        V(*flat), V(*flat), V(*strip), V(*strip),
        V(*flat), V(*flat), V(*strip), V(*strip),
        V(max(rows - 1, 1), cols, piece, win), V(cols, piece, win),
        V(max(cols - 1, 1), piece, win), V(*split_shape),
        dma((6,)), dma((2, 2, 8)), dma((2, 2, 8)),
        dma((2, max(rows - 1, 1))), dma((2, max(rows - 1, 1))),
        dma((2, max(cols - 1, 1))), dma((2, max(cols - 1, 1))),
    ]
    new_obj, new_probe, part = pl.pallas_call(
        functools.partial(kernel, rows, cols),
        out_shape=(
            jax.ShapeDtypeStruct(objects.shape, f32),
            jax.ShapeDtypeStruct(split_shape, f32),
            jax.ShapeDtypeStruct(probe.shape, f32),
        ),
        in_specs=[smem, smem] + [anyspace] * 6,
        out_specs=(vmem, vmem, vmem),
        scratch_shapes=scratch,
        compiler_params=pltpu.CompilerParams(
            collective_id=0, has_side_effects=True, vmem_limit_bytes=56 * 2**20
        ),
    )(
        offsets.reshape(2), counts.reshape(1), objects, prev_partial.reshape(split_shape),
        probe, probe.reshape(split_shape), amplitudes.reshape(win, win), table,
    )
    return new_obj, new_probe.reshape(probe.shape), part[None, None]


def solution(mesh):
    in_specs = (
        P(None, None, "row", "col"),
        P(),
        P("row", "col", None, None, None),
        P("row", "col", None, None),
        P("row", "col"),
        P("row", "col", None, None, None),
    )
    out_specs = (P(None, None, "row", "col"), P(), P("row", "col", None, None, None))
    body = functools.partial(shards, mesh.shape["row"], mesh.shape["col"])
    return jax.shard_map(body, mesh=mesh, in_specs=in_specs, out_specs=out_specs, check_vma=False)
```

```python
import functools
import math

import jax
import jax.numpy as jnp
import numpy as np
from jax import lax
from jax.experimental import pallas as pl
from jax.experimental.pallas import tpu as pltpu
from jax.sharding import PartitionSpec as P

HALO = 64
OBJ_RATE = 0.1
PROBE_RATE = 0.3
MESH = pl.DeviceIdType.MESH

STEPS = ((-1, 0), (1, 0), (0, -1), (0, 1), (-1, -1), (-1, 1), (1, -1), (1, 1))


def split(value):
    high = value.astype(jnp.bfloat16)
    low = (value - high.astype(jnp.float32)).astype(jnp.bfloat16)
    return high, low


def operator_table(n):
    index = np.arange(n)
    angle = 2.0 * np.pi * (np.outer(index, index) % n) / n
    dft = np.exp(-1j * angle) / np.sqrt(n)
    freq = np.where(index < n // 2, index, index - n).astype(np.float64)
    phase = np.exp(1j * np.pi * freq * freq / (4.0 * n))
    prop = np.conj(dft) @ (phase[:, None] * dft)
    tables = []
    for mat in (dft, prop):
        for part in (mat.real, mat.imag, -mat.imag):
            part = part.astype(np.float32)
            high = part.astype(jnp.bfloat16)
            low = (part - high.astype(np.float32)).astype(jnp.bfloat16)
            tables += [high, low]
    return np.stack(tables).reshape(2, 3, 2, n, n)


def dot(left, right):
    return jnp.dot(left, right, preferred_element_type=jnp.float32)


def cat(parts, axis):
    return jnp.concatenate(parts, axis=axis)


def sandwich(xr, xi, table, which, conj):
    re, im, neg = table.at[which, 0], table.at[which, 1], table.at[which, 2]
    if conj:
        im, neg = neg, im
    rh, rl, ih, il, nh, nl = (p[k] for p in (re, im, neg) for k in (0, 1))
    n = xr.shape[0]
    high, low = split(cat([xr, xi], 0))
    left = cat([high, low, high], 1)
    by_re = dot(left, cat([rh, rh, rl], 0))
    by_im = dot(left, cat([ih, ih, il], 0))
    trh, trl = split(by_re[:n] - by_im[n:])
    tih, til = split(by_im[:n] + by_re[n:])
    right = cat([trh, tih, trl, til, trh, tih], 0)
    left = cat([cat([rh, nh, rh, nh, rl, nl], 1), cat([ih, rh, ih, rh, il, rl], 1)], 0)
    both = dot(left, right)
    yr, yi = both[:n], both[n:]
    return yr, yi


def kernel(
    rows, cols, offs, count, obj_hbm, prev_hbm, probe_hbm, probe_k_hbm, amp_hbm, table_hbm,
    out_obj, out_probe, out_part,
    obj, prev, probe, probe_piece, amp, table,
    pw, pe, ext, rw, re_,
    acc, gn, gs, gw_, ge, qn, qs, qw, qe,
    buf1, sum1, buf2, newp, part_buf,
    local_sem, halo_send, halo_recv, row_send, row_recv, col_send, col_recv,
):
    tile = obj.shape[2]
    win = probe.shape[1]
    side = tile + 2 * HALO
    row, col = lax.axis_index("row"), lax.axis_index("col")

    def exists(dr, dc):
        r, c = row + dr, col + dc
        return (r >= 0) & (r < rows) & (c >= 0) & (c < cols)

    fetches = [
        pltpu.make_async_copy(src, dst, local_sem.at[k])
        for k, (src, dst) in enumerate(
            ((obj_hbm, obj), (prev_hbm, prev), (probe_k_hbm.at[row, col], probe_piece),
             (probe_hbm, probe), (table_hbm, table), (amp_hbm, amp))
        )
    ]
    for fetch in fetches:
        fetch.start()

    barrier = pltpu.get_barrier_semaphore()

    def greet(r, c):
        pl.semaphore_signal(barrier, inc=1, device_id=(r, c), device_id_type=MESH)

    for t in range(1, rows):
        greet(lax.rem(row + t, rows), col)
    for t in range(1, cols):
        greet(row, lax.rem(col + t, cols))
    for dr, dc in STEPS[4:]:
        @pl.when(exists(dr, dc))
        def _():
            greet(row + dr, col + dc)

    lane = lax.broadcasted_iota(jnp.int32, (1, 2 * HALO), 1)
    first = lane < HALO

    def swap(value):
        return pltpu.roll(value, HALO, 1)

    fetches[0].wait()
    for s in range(2):
        head_re, head_im = obj[s, 0, :, : 2 * HALO], obj[s, 1, :, : 2 * HALO]
        tail_re, tail_im = obj[s, 0, :, tile - 2 * HALO :], obj[s, 1, :, tile - 2 * HALO :]
        pw[s] = jnp.where(first, head_re, swap(head_im))
        pe[s] = jnp.where(first, swap(tail_re), tail_im)

    north, south = pl.ds(0, HALO), pl.ds(tile + HALO, HALO)
    middle = pl.ds(HALO, tile)
    low, high = pl.ds(0, HALO), pl.ds(tile - HALO, HALO)
    wide = pl.ds(0, tile)

    def halo_plan(s):
        return (
            (obj.at[s, :, low, :], ext.at[s, :, south, wide]),
            (obj.at[s, :, high, :], ext.at[s, :, north, wide]),
            (pw.at[s], re_.at[s, middle]),
            (pe.at[s], rw.at[s, middle]),
            (pw.at[s, low], re_.at[s, south]),
            (pe.at[s, low], rw.at[s, south]),
            (pw.at[s, high], re_.at[s, north]),
            (pe.at[s, high], rw.at[s, north]),
        )

    def grad_plan(s):
        return (
            (gn.at[s], qs.at[s]),
            (gs.at[s], qn.at[s]),
            (gw_.at[s, middle], qe.at[s, middle]),
            (ge.at[s, middle], qw.at[s, middle]),
            (gw_.at[s, north], qe.at[s, south]),
            (ge.at[s, north], qw.at[s, south]),
            (gw_.at[s, south], qe.at[s, north]),
            (ge.at[s, south], qw.at[s, north]),
        )

    def plan_of(phase, s):
        return halo_plan(s) if phase == 0 else grad_plan(s)

    def copies(phase, s):
        plan = plan_of(phase, s)
        return [
            (dr, dc, dst, pltpu.make_async_remote_copy(
                src_ref=src, dst_ref=dst,
                send_sem=halo_send.at[phase, s, d], recv_sem=halo_recv.at[phase, s, d],
                device_id=(row + dr, col + dc), device_id_type=MESH))
            for d, ((dr, dc), (src, dst)) in enumerate(zip(STEPS, plan))
        ]

    order = (2, 3, 4, 5, 6, 7, 0, 1)

    def send(phase, s):
        todo = copies(phase, s)
        for d in order:
            dr, dc, dst, copy = todo[d]

            @pl.when(exists(dr, dc))
            def _():
                copy.start()

    def blank(phase, s):
        for (dr, dc), (_, dst) in zip(STEPS, plan_of(phase, s)):
            @pl.when(jnp.logical_not(exists(-dr, -dc)))
            def _():
                dst[...] = jnp.zeros(dst.shape, jnp.float32)

    def arrive(phase, s):
        for dr, dc, dst, copy in copies(phase, s):
            @pl.when(exists(-dr, -dc))
            def _():
                copy.wait_recv()

    def sent(phase, s):
        for dr, dc, dst, copy in copies(phase, s):
            @pl.when(exists(dr, dc))
            def _():
                copy.wait_send()

    def row_copies(stage):
        made = []
        for t in range(1, rows):
            peer = lax.rem(row + t, rows)
            if stage == 0:
                src, dst = prev.at[peer], buf1.at[t - 1]
            else:
                src, dst = newp.at[row], newp.at[row]
            made.append(pltpu.make_async_remote_copy(
                src_ref=src, dst_ref=dst, send_sem=row_send.at[stage, t - 1],
                recv_sem=row_recv.at[stage, t - 1], device_id=(peer, col), device_id_type=MESH))
        return made

    def col_copies(stage):
        made = []
        for t in range(1, cols):
            peer = lax.rem(col + t, cols)
            if stage == 0:
                src, dst = sum1.at[peer], buf2.at[t - 1]
            else:
                src, dst = newp.at[row, col], newp.at[row, col]
            made.append(pltpu.make_async_remote_copy(
                src_ref=src, dst_ref=dst, send_sem=col_send.at[stage, t - 1],
                recv_sem=col_recv.at[stage, t - 1], device_id=(row, peer), device_id_type=MESH))
        return made

    diagonals = sum(exists(dr, dc).astype(jnp.int32) for dr, dc in STEPS[4:])
    pl.semaphore_wait(barrier, rows - 1 + cols - 1 + diagonals)

    send(0, 0)
    fetches[1].wait()
    rs_rows = row_copies(0)
    for copy in rs_rows:
        copy.start()
    send(0, 1)

    for s in range(2):
        for part in range(2):
            ext[s, part, HALO : HALO + tile, :] = obj[s, part]
        blank(0, s)
        blank(1, s)

    for copy in rs_rows:
        copy.wait_recv()
    total = prev[row]
    for t in range(1, rows):
        total = total + buf1[t - 1]
    sum1[...] = total
    rs_cols = col_copies(0)
    for copy in rs_cols:
        copy.start()

    top, left = offs[0], offs[1]

    def one_hot(shape, axis, shift):
        longer = lax.broadcasted_iota(jnp.int32, shape, axis)
        shorter = lax.broadcasted_iota(jnp.int32, shape, 1 - axis) + shift
        shorter = jnp.where(shorter < 0, shorter + side, shorter)
        return (longer == shorter).astype(jnp.float32).astype(jnp.bfloat16)

    def twice(value, axis):
        return cat([value, value], axis)

    def window(s):
        east, west = re_[s], rw[s]
        full = cat([
            ext[s, 0, :, :tile], jnp.where(first, east, swap(west)),
            ext[s, 1, :, :tile], jnp.where(first, swap(east), west),
        ], 1)
        pick_rows = one_hot((win, side), 1, top)
        pick_cols = one_hot((side, win), 0, left - HALO)
        some = dot(twice(pick_rows, 1), cat(split(full), 0))
        some = cat([some[:, :side], some[:, side:]], 0)
        some = dot(cat(split(some), 1), twice(pick_cols, 0))
        return some[:win], some[win:]

    def place(s, gre, gim):
        put_cols = one_hot((win, side), 1, left - HALO)
        put_rows = one_hot((side, win), 0, top)
        some = dot(cat(split(cat([gre, gim], 0)), 1), twice(put_cols, 0))
        some = cat([some[:win], some[win:]], 1)
        full = dot(twice(put_rows, 1), cat(split(some), 0))
        full_re, full_im = full[:, :side], full[:, side:]
        for part, value in enumerate((full_re, full_im)):
            gn[s, part] = value[:HALO, :tile]
            gs[s, part] = value[HALO + tile :, :tile]
            acc[s, part] = value[HALO : HALO + tile, :tile]
        edge_re, edge_im = full_re[:, tile:], full_im[:, tile:]
        ge[s] = jnp.where(first, edge_re, swap(edge_im))
        gw_[s] = jnp.where(first, swap(edge_re), edge_im)

    arrive(0, 0)
    for k in (3, 4):
        fetches[k].wait()
    ar, ai = window(0)
    pr, pi = probe[0], probe[1]
    vr, vi = sandwich(pr * ar - pi * ai, pr * ai + pi * ar, table, 1, False)

    for copy in rs_cols:
        copy.wait_recv()
    fetches[2].wait()
    total = sum1[col]
    for t in range(1, cols):
        total = total + buf2[t - 1]
    rate = PROBE_RATE / math.sqrt(rows * cols)
    newp[row, col] = probe_piece[...] - rate * total
    ag_cols = col_copies(1)
    for copy in ag_cols:
        copy.start()

    arrive(0, 1)
    br, bi = window(1)
    wr, wi = sandwich(vr * br - vi * bi, vr * bi + vi * br, table, 0, False)
    fetches[5].wait()
    live = jnp.where(count[0] > 0, 2.0, 0.0)
    scale = live * (1.0 - amp[...] / jnp.sqrt(wr * wr + wi * wi + 1.0))
    xr, xi = sandwich(scale * wr, scale * wi, table, 0, True)
    place(1, xr * vr + xi * vi, xi * vr - xr * vi)
    send(1, 1)

    for copy in ag_cols:
        copy.wait_recv()
    ag_rows = row_copies(1)
    for copy in ag_rows:
        copy.start()

    ur, ui = sandwich(xr * br + xi * bi, xi * br - xr * bi, table, 1, True)
    place(0, ur * pr + ui * pi, ui * pr - ur * pi)
    send(1, 0)
    part_buf[0] = ur * ar + ui * ai
    part_buf[1] = ui * ar - ur * ai
    writes = [
        pltpu.make_async_copy(src, dst, local_sem.at[6 + k])
        for k, (src, dst) in enumerate(
            ((part_buf, out_part), (newp, out_probe), (acc.at[1], out_obj.at[1]), (acc.at[0], out_obj.at[0]))
        )
    ]
    writes[0].start()

    def finish(s):
        arrive(1, s)
        top_strip, bottom_strip = slice(0, HALO), slice(tile - HALO, tile)
        for part in range(2):
            acc[s, part, top_strip, :] += qn[s, part]
            acc[s, part, bottom_strip, :] += qs[s, part]
        for q, near, lanes in ((qw, True, slice(0, 2 * HALO)), (qe, False, slice(tile - 2 * HALO, tile))):
            for src, dst in (
                (slice(HALO, HALO + tile), slice(0, tile)),
                (slice(0, HALO), top_strip),
                (slice(HALO + tile, side), bottom_strip),
            ):
                value = q[s, src]
                turned = swap(value)
                if near:
                    acc[s, 0, dst, lanes] += jnp.where(first, value, 0.0)
                    acc[s, 1, dst, lanes] += jnp.where(first, turned, 0.0)
                else:
                    acc[s, 0, dst, lanes] += jnp.where(first, 0.0, turned)
                    acc[s, 1, dst, lanes] += jnp.where(first, 0.0, value)
        for part in range(2):
            acc[s, part] = obj[s, part] - OBJ_RATE * acc[s, part]

    for copy in ag_rows:
        copy.wait_recv()
    writes[1].start()
    finish(1)
    writes[2].start()
    finish(0)
    writes[3].start()

    for s in range(2):
        sent(0, s)
        sent(1, s)
    for copy in rs_rows + rs_cols + ag_cols + ag_rows:
        copy.wait_send()
    for write in writes:
        write.wait()


def shards(rows, cols, objects, probe, prev_partial, offsets, counts, amplitudes):
    tile = objects.shape[2]
    win = probe.shape[-1]
    side = tile + 2 * HALO
    piece = (2 * win) // (rows * cols)
    split_shape = (rows, cols, piece, win)
    table = jnp.asarray(operator_table(win))
    f32 = jnp.float32
    smem = pl.BlockSpec(memory_space=pltpu.SMEM)
    anyspace = pl.BlockSpec(memory_space=pl.ANY)
    V = lambda *shape: pltpu.VMEM(shape, f32)
    strip = (2, side, 2 * HALO)
    flat = (2, 2, HALO, tile)
    dma = pltpu.SemaphoreType.DMA
    scratch = [
        V(2, 2, tile, tile), V(*split_shape), V(2, win, win), V(piece, win), V(win, win),
        pltpu.VMEM(table.shape, jnp.bfloat16),
        V(2, tile, 2 * HALO), V(2, tile, 2 * HALO), V(2, 2, side, tile), V(*strip), V(*strip),
        V(2, 2, tile, tile),
        V(*flat), V(*flat), V(*strip), V(*strip),
        V(*flat), V(*flat), V(*strip), V(*strip),
        V(max(rows - 1, 1), cols, piece, win), V(cols, piece, win),
        V(max(cols - 1, 1), piece, win), V(*split_shape), V(2, win, win),
        dma((10,)), dma((2, 2, 8)), dma((2, 2, 8)),
        dma((2, max(rows - 1, 1))), dma((2, max(rows - 1, 1))),
        dma((2, max(cols - 1, 1))), dma((2, max(cols - 1, 1))),
    ]
    new_obj, new_probe, part = pl.pallas_call(
        functools.partial(kernel, rows, cols),
        out_shape=(
            jax.ShapeDtypeStruct(objects.shape, f32),
            jax.ShapeDtypeStruct(split_shape, f32),
            jax.ShapeDtypeStruct(probe.shape, f32),
        ),
        in_specs=[smem, smem] + [anyspace] * 6,
        out_specs=(anyspace,) * 3,
        scratch_shapes=scratch,
        compiler_params=pltpu.CompilerParams(
            collective_id=0, has_side_effects=True, vmem_limit_bytes=56 * 2**20
        ),
    )(
        offsets.reshape(2), counts.reshape(1), objects, prev_partial.reshape(split_shape),
        probe, probe.reshape(split_shape), amplitudes.reshape(win, win), table,
    )
    return new_obj, new_probe.reshape(probe.shape), part[None, None]


def solution(mesh):
    in_specs = (
        P(None, None, "row", "col"),
        P(),
        P("row", "col", None, None, None),
        P("row", "col", None, None),
        P("row", "col"),
        P("row", "col", None, None, None),
    )
    out_specs = (P(None, None, "row", "col"), P(), P("row", "col", None, None, None))
    body = functools.partial(shards, mesh.shape["row"], mesh.shape["col"])
    return jax.shard_map(body, mesh=mesh, in_specs=in_specs, out_specs=out_specs, check_vma=False)
```
